128 devices in a mesh: corpus: 32 (over y, z, core), tensor: 4 (over x).
Axes of the slice: x: 4, y: 4, z: 4, core: 2. Of those that a mesh axis runs over, the one named last changes fastest.
Arguments:
- hidden: bfloat16 [12288, 4096], P('corpus', 'tensor'), may hold values from -6 to 6
- lengths: int32 [32, 32], P('corpus'), may hold values from 1 to 48, 384 in all within a row
- steer_ids: int32 [1024], P('corpus'), may hold values from 0 to 15
- in_gain: float32 [4096], replicated, may hold values from 0.6 to 14
- w_query: bfloat16 [4096, 2048], P(None, 'tensor'), may hold values from -0.09375 to 0.09375
- w_key: bfloat16 [4096, 1024], P(None, 'tensor'), may hold values from -0.09375 to 0.09375
- w_value: bfloat16 [4096, 1024], P(None, 'tensor'), may hold values from -0.09375 to 0.09375
- w_out: bfloat16 [2048, 4096], P('tensor'), may hold values from -0.125 to 0.125
- steer_table: bfloat16 [16, 4096], replicated, may hold values from -12 to 12
- strength: float32 [16], replicated, may hold values from 0.1 to 0.5
- out_gain: float32 [4096], replicated, may hold values from 0.1 to 1.9
- index_rows: bfloat16 [131072, 4096], P(('corpus', 'tensor')), may hold values from -6 to 6
Outputs:
- scores: bfloat16 [1024, 131072], P(None, ('corpus', 'tensor'))
The draws below stay inside these ranges and needn't reach their ends.
Inputs may be any that keep to these rules, and one draw needn't show every extreme that they name: Each row of lengths holds the token counts of the 32 queries packed in order into the 384 tokens of one group.
All inputs are finite; a program needn't handle non-finite values.
Results may differ from the reference program's by a relative error of at most 0.005.
The reference program's roundings to bfloat16 on the way count: a program that leaves them out, or rounds other values in their place, can miss the bound.
Values may be sent and summed in bfloat16 or wider, within the bound.
No kernel may reach another device: no remote copies, remote signals or barrier semaphores. Data moves between devices by JAX's collectives and lax.ppermute only.
A program may use at most 128 MiB of HBM per device.

```python
import math
import jax
import jax.numpy as jnp
import numpy as np
from jax import lax

D = 4096
HEADS = 16
KV_HEADS = 8
HEAD = 128
TOK_DEV = 384
QUERY_DEV = 32
IDX_DEV = 1024
MAXLEN = 48
STEER = 16
GROUPS = 32
TOKENS = 12288
QUERIES = 1024
INDEX = 131072


def draw_in_gain(key, part):
    return jax.random.uniform(key, (D,), jnp.float32, 0.6, 1.4)


def draw_steer_table(key, part):
    along = jnp.arange(D, dtype=jnp.float32) / D
    spread = 0.3 * 10.0 ** along
    base = jax.random.truncated_normal(key, -4.0, 4.0, (STEER, D), jnp.float32)
    return (base * spread[None, :]).astype(jnp.bfloat16)


def with_ends(entries, stream_key, smallest, high):
    index_at = [jax.random.randint(jax.random.fold_in(stream_key, axis), (), 0, length) for axis, length in enumerate(entries.shape)]
    longest = entries.shape.index(max(entries.shape))
    neighbour = index_at[:longest] + [(index_at[longest] + 1) % entries.shape[longest]] + index_at[longest + 1:]
    return entries.at[tuple(index_at)].set(smallest).at[tuple(neighbour)].set(high)


def levels(key, dims, shards, smallest, high):
    loudness = 1.0
    for position, parts in shards:
        heights = jax.random.uniform(jax.random.fold_in(jax.random.fold_in(key, 6), position), (parts,), jnp.float32, smallest / len(shards), high / len(shards))
        loudness = loudness * jnp.repeat(jnp.exp(heights), dims[position] // parts).reshape((-1,) + (1,) * (len(dims) - 1 - position))
    return loudness


def profile(number_of, total, reach, lean):
    loads = [(1 << 20) // math.isqrt(rank ** lean) + 1 for rank in range(2, number_of + 1)]
    surplus, counts = total - reach - (number_of - 1), [1] * (number_of - 1)
    while surplus > 0:
        free = [i for i in range(number_of - 1) if counts[i] < reach]
        pool, remaining = sum([loads[i] for i in free]), surplus
        for i in free:
            more = min(reach - counts[i], max(1, remaining * loads[i] // pool), surplus)
            counts[i] = counts[i] + more
            surplus = surplus - more
    return np.array([reach] + counts)


def uneven(stream_key, count, total, bound, lean):
    if count == 2:
        one = jax.random.randint(stream_key, (), max(1, total - bound), min(bound, total - 1) + 1)
        return jnp.stack([one, total - one])
    tallies = jnp.asarray(profile(count, total, bound, lean), jnp.int32)
    couples = (count - 1) // 2
    source_of, receiver = tallies[1:1 + 2 * couples:2], tallies[2:2 + 2 * couples:2]
    room = jnp.minimum(source_of - 1, bound - receiver)
    shifted = jax.random.randint(jax.random.fold_in(stream_key, 1), (couples,), 0, 1 << 20) % (room + 1)
    tallies = tallies.at[1:1 + 2 * couples:2].set(source_of - shifted).at[2:2 + 2 * couples:2].set(receiver + shifted)
    return tallies[jax.random.permutation(jax.random.fold_in(stream_key, 2), count)]


def scatter_about(rng, extent, deviation, reach, pieces=(), kind=jnp.bfloat16):
    entries = jax.random.normal(rng, extent, jnp.float32) * deviation
    if len(pieces) > 0:
        entries = levels(rng, extent, pieces, -0.22, 0.18) * entries
    return jnp.clip(entries, min=-reach, max=reach).astype(kind)


def setup_inputs(seed: int = 0) -> dict:
    splits = jax.random.split(jax.random.key(seed), 13)
    hidden = scatter_about(splits[0], (TOKENS, D), 1.0, 6.0, ((0, 32), (1, 4)))
    lengths = jax.vmap(lambda own: uneven(own, QUERY_DEV, TOK_DEV, MAXLEN, 2))(jax.random.split(splits[1], GROUPS)).reshape((GROUPS, QUERY_DEV)).astype(jnp.int32)
    steer_ids = with_ends(jax.random.randint(splits[2], (QUERIES,), 0, STEER), jax.random.fold_in(splits[2], 1), 0, STEER - 1).astype(jnp.int32)
    in_gain = draw_in_gain(jax.random.fold_in(splits[12], 71), 0)
    w_query = scatter_about(splits[4], (D, HEADS * HEAD), D ** -0.5, 0.09375, ((1, 4),))
    w_key = scatter_about(splits[5], (D, KV_HEADS * HEAD), D ** -0.5, 0.09375, ((1, 4),))
    w_value = scatter_about(splits[6], (D, KV_HEADS * HEAD), D ** -0.5, 0.09375, ((1, 4),))
    w_out = scatter_about(splits[7], (HEADS * HEAD, D), (HEADS * HEAD) ** -0.5, 0.125, ((0, 4),))
    steer_table = draw_steer_table(jax.random.fold_in(splits[12], 71), 0)
    strength = jnp.clip(jnp.exp(jax.random.uniform(splits[9], (STEER,), jnp.float32, math.log(0.1), math.log(0.5))), 0.1, 0.5)
    out_gain = jnp.clip(1.0 + 0.18 * jax.random.normal(splits[10], (D,), jnp.float32), 0.1, 1.9)
    index_rows = scatter_about(splits[11], (INDEX, D), 1.0, 6.0, ((0, 128),))
    return dict(hidden=hidden, lengths=lengths, steer_ids=steer_ids, in_gain=in_gain, w_query=w_query, w_key=w_key, w_value=w_value, w_out=w_out, steer_table=steer_table, strength=strength, out_gain=out_gain, index_rows=index_rows)


rope_base = 1000000.0

def rotate(vectors, positions):
    half_width = vectors.shape[-1] // 2
    frequency = rope_base ** (-(jnp.arange(half_width, dtype=jnp.float32) * 2.0) / vectors.shape[-1])
    angles = positions.astype(jnp.float32)[:, None] * frequency[None, :]
    cosine = jnp.cos(angles)[:, None, :]
    sine_part = jnp.sin(angles)[:, None, :]
    leading = vectors[..., :half_width]
    second = vectors[..., half_width:]
    return jnp.concatenate([leading * cosine - second * sine_part, second * cosine + leading * sine_part], axis=-1)

def encode(normed, lengths_row, w_query, w_key, w_value):
    tok_count = normed.shape[0]
    query_count = lengths_row.shape[0]
    seq_ends = jnp.cumsum(lengths_row).astype(jnp.int32)
    starts = seq_ends - lengths_row
    places = jnp.arange(tok_count, dtype=jnp.int32)
    owners = lax.optimization_barrier(jnp.sum((places[:, None] >= seq_ends[None, :]).astype(jnp.int32), axis=1))
    positions = places - jnp.take(starts, owners)
    finals = seq_ends - 1
    pooled = jnp.take(normed, finals, axis=0)
    kv_heads = w_key.shape[1] // HEAD
    q_heads = w_query.shape[1] // HEAD
    group_size = q_heads // kv_heads
    key_rows = jnp.dot(normed, w_key, preferred_element_type=jnp.float32).reshape(tok_count, kv_heads, HEAD)
    key_rows = rotate(key_rows, positions).astype(jnp.bfloat16)
    values = jnp.dot(normed, w_value, preferred_element_type=jnp.float32).astype(jnp.bfloat16).reshape(tok_count, kv_heads, HEAD)
    queries = jnp.dot(pooled, w_query, preferred_element_type=jnp.float32).reshape(query_count, q_heads, HEAD)
    queries = rotate(queries, lengths_row - 1).astype(jnp.bfloat16).reshape(query_count, kv_heads, group_size, HEAD)
    scores = jnp.einsum('qgrd,tgd->grqt', queries.astype(jnp.float32), key_rows.astype(jnp.float32)) * HEAD ** (-0.5)
    visible = owners[None, None, None, :] == jnp.arange(query_count, dtype=jnp.int32)[None, None, :, None]
    scores = jnp.where(visible, scores, -1e+30)
    maxima = lax.optimization_barrier(jnp.max(scores, axis=3, keepdims=True))
    weights = jnp.exp(scores - maxima)
    attn_probs = (weights / lax.optimization_barrier(jnp.sum(weights, axis=3, keepdims=True))).astype(jnp.bfloat16)
    context = jnp.einsum('grqt,tgd->qgrd', attn_probs.astype(jnp.float32), values.astype(jnp.float32))
    context = context.astype(jnp.bfloat16).reshape(query_count, q_heads * HEAD)
    return (context, finals)

def steer_finish(residual, steering, scaled, out_gain):
    self_sq = lax.optimization_barrier(jnp.sum(residual * residual, axis=1))
    steer_sq = lax.optimization_barrier(jnp.sum(steering * steering, axis=1))
    factor = scaled * jnp.sqrt(self_sq / D / (steer_sq / D + 1e-06))
    gained = (residual + factor[:, None] * steering) * out_gain[None, :]
    totals = lax.optimization_barrier(jnp.sum(gained * gained, axis=1, keepdims=True))
    return (gained * lax.rsqrt(totals + 1e-06)).astype(jnp.bfloat16)

def reference(hidden, lengths, steer_ids, in_gain, w_query, w_key, w_value, w_out, steer_table, strength, out_gain, index_rows):
    grouped = hidden.reshape(GROUPS, TOK_DEV, D)
    picked_all = steer_ids.reshape(GROUPS, QUERY_DEV)

    def one_group(group_args):
        group_rows, lengths_row, picked = group_args
        widened = group_rows.astype(jnp.float32)
        normed = (widened * lax.rsqrt(lax.optimization_barrier(jnp.mean(widened * widened, axis=1, keepdims=True)) + 1e-06) * in_gain[None, :]).astype(jnp.bfloat16)
        context, finals = encode(normed, lengths_row, w_query, w_key, w_value)
        attn_out = jnp.dot(context, w_out, preferred_element_type=jnp.float32)
        residual = jnp.take(widened, finals, axis=0) + attn_out
        steering = jnp.take(steer_table, picked, axis=0).astype(jnp.float32)
        scaled = jnp.take(strength, picked)
        return steer_finish(residual, steering, scaled, out_gain)
    embeddings = lax.map(one_group, (grouped, lengths, picked_all)).reshape(QUERIES, D)
    blocks = index_rows.reshape(INDEX // IDX_DEV, IDX_DEV, D)

    def score_block(index_block):
        return jnp.dot(embeddings, index_block.T, preferred_element_type=jnp.float32).astype(jnp.bfloat16)
    scored = lax.map(score_block, blocks)
    return jnp.transpose(scored, (1, 0, 2)).reshape(QUERIES, INDEX)
```

```python
import jax
import jax.numpy as jnp
from jax import lax
from jax.experimental import pallas as pl
from jax.experimental.pallas import tpu as pltpu
from jax.sharding import PartitionSpec as P

D = 4096
HEAD = 128
TOK = 384
QRY = 32
ROPE_BASE = 1000000.0
BF = jnp.bfloat16
F32 = jnp.float32


VM = pl.BlockSpec(memory_space=pltpu.VMEM)
SM = pl.BlockSpec(memory_space=pltpu.SMEM)
ANY = pl.BlockSpec(memory_space=pl.ANY)


def ring(k):
    return [(i, (i + k) % 4) for i in range(4)]


def spot(y, z, core):
    return ((y % 4) * 4 + z % 4) * 2 + core


def planes(first, k):
    pairs = []
    for y in range(4):
        for z in range(4):
            for core in range(2):
                along_y = (core == 0) == first
                target = spot(y + k, z, core) if along_y else spot(y, z + k, core)
                pairs.append((spot(y, z, core), target))
    return pairs


def partners():
    return [(i, i ^ 1) for i in range(32)]


def rotary(positions):
    half = HEAD // 2
    frequency = ROPE_BASE ** (-(jnp.arange(half, dtype=F32) * 2.0) / HEAD)
    frequency = jnp.concatenate([frequency, frequency])
    sign = jnp.where(jnp.arange(HEAD) < half, -1.0, 1.0).astype(F32)
    angles = positions.astype(F32)[:, None] * frequency[None, :]
    return jnp.cos(angles), jnp.sin(angles) * sign[None, :]


def encode_kernel(
    meta,
    own,
    left,
    right,
    far_top,
    far_low,
    gain,
    cos_k,
    sin_k,
    cos_q,
    sin_q,
    starts,
    ends,
    my_ends,
    wq_hbm,
    wk_hbm,
    wv_hbm,
    wo_hbm,
    part0,
    part1,
    part2,
    part3,
    pooled_x,
    normed,
    wq,
    wk,
    wv,
    wo,
    context,
    summed,
    sems,
):
    width = own.shape[1]
    copies = []
    for i, (source, target) in enumerate(((wk_hbm, wk), (wv_hbm, wv), (wq_hbm, wq))):
        for j in range(4):
            rows = pl.ds(pl.multiple_of(meta[j] * width, width), width)
            copies.append(
                pltpu.make_async_copy(source.at[rows], target.at[pl.ds(j * width, width)], sems.at[i * 4 + j])
            )
    copies.append(pltpu.make_async_copy(wo_hbm, wo, sems.at[12]))
    for copy in copies:
        copy.start()

    chunk = 64
    for base in range(0, TOK, chunk):
        if base < TOK // 2:
            far, far_base = far_top, base
        else:
            far, far_base = far_low, base - TOK // 2
        blocks = [(own, base), (left, base), (right, base), (far, far_base)]
        acc = jnp.zeros((chunk, 128), F32)
        for ref, start in blocks:
            for lane in range(0, width, 128):
                x = ref[start : start + chunk, lane : lane + 128].astype(F32)
                acc = acc + x * x
        scale = lax.rsqrt(jnp.sum(acc, axis=1, keepdims=True) / D + 1e-06)
        for j, (ref, start) in enumerate(blocks):
            x = ref[start : start + chunk, :].astype(F32)
            row = gain[pl.ds(meta[j], 1), :]
            normed[base : base + chunk, j * width : (j + 1) * width] = (x * scale * row).astype(BF)

    tokens = lax.broadcasted_iota(jnp.int32, (QRY, TOK), 1)
    visible = (tokens >= starts[...]) & (tokens < ends[...])
    pick = (tokens == ends[...] - 1).astype(F32).astype(BF)

    half_tokens = lax.broadcasted_iota(jnp.int32, (8, TOK // 2), 1)
    last8 = my_ends[...] - 1
    pick8_top = (half_tokens == last8).astype(F32).astype(BF)
    pick8_low = (half_tokens + TOK // 2 == last8).astype(F32).astype(BF)
    half = TOK // 2
    raw = [
        (own[0:half, :], own[half:TOK, :]),
        (left[0:half, :], left[half:TOK, :]),
        (right[0:half, :], right[half:TOK, :]),
        (far_top[...], far_low[...]),
    ]
    for j, (top, low) in enumerate(raw):
        rows = jnp.dot(pick8_top, top, preferred_element_type=F32) + jnp.dot(
            pick8_low, low, preferred_element_type=F32
        )
        pooled_x[:, pl.ds(pl.multiple_of(meta[j] * width, width), width)] = rows

    for copy in copies[0:4]:
        copy.wait()
    keys = jnp.dot(normed[...], wk[...], preferred_element_type=F32)
    for copy in copies[4:8]:
        copy.wait()
    values = jnp.dot(normed[...], wv[...], preferred_element_type=F32).astype(BF)
    pooled = jnp.dot(pick, normed[...], preferred_element_type=F32).astype(BF)
    for copy in copies[8:12]:
        copy.wait()
    queries = jnp.dot(pooled, wq[...], preferred_element_type=F32)

    def turn(v, cosine, sine):
        return (v * cosine + pltpu.roll(v, HEAD // 2, 1) * sine).astype(BF)

    for g in range(2):
        lanes = slice(g * HEAD, (g + 1) * HEAD)
        key = turn(keys[:, lanes], cos_k[...], sin_k[...])
        value = values[:, lanes]
        for r in range(2):
            h = 2 * g + r
            heads = slice(h * HEAD, (h + 1) * HEAD)
            query = turn(queries[:, heads], cos_q[...], sin_q[...])
            scores = lax.dot_general(
                query, key, (((1,), (1,)), ((), ())), preferred_element_type=F32
            ) * HEAD ** (-0.5)
            scores = jnp.where(visible, scores, -1e30)
            weights = jnp.exp(scores - jnp.max(scores, axis=1, keepdims=True))
            probs = (weights / jnp.sum(weights, axis=1, keepdims=True)).astype(BF)
            context[:, heads] = jnp.dot(probs, value, preferred_element_type=F32).astype(BF)

    copies[12].wait()
    summed[...] = jnp.dot(context[...], wo[...], preferred_element_type=F32)
    for k, part in enumerate((part0, part1, part2, part3)):
        first = lax.rem(meta[4] + k, 4) * 8
        part[...] = summed[pl.ds(pl.multiple_of(first, 8), 8), :]


def encode(meta, blocks, gain, tables, bounds, weights):
    rows = jax.ShapeDtypeStruct((8, D), F32)
    return pl.pallas_call(
        encode_kernel,
        in_specs=[SM] + [VM] * 5 + [VM] + [VM] * 4 + [VM] * 3 + [ANY] * 4,
        out_specs=[VM] * 5,
        out_shape=[rows] * 5,
        scratch_shapes=[
            pltpu.VMEM((TOK, D), BF),
            pltpu.VMEM((D, 512), BF),
            pltpu.VMEM((D, 256), BF),
            pltpu.VMEM((D, 256), BF),
            pltpu.VMEM((512, D), BF),
            pltpu.VMEM((QRY, 512), BF),
            pltpu.VMEM((QRY, D), F32),
            pltpu.SemaphoreType.DMA((13,)),
        ],
        compiler_params=pltpu.CompilerParams(vmem_limit_bytes=36 << 20),
        name="encode",
    )(meta, *blocks, gain, *tables, *bounds, *weights)


def embed_kernel(part0, part1, part2, part3, pooled_x, ids, table, strength, gain, out):
    residual = pooled_x[...] + ((part0[...] + part1[...]) + (part2[...] + part3[...]))
    one_hot = ids[...] == lax.broadcasted_iota(jnp.int32, (8, 16), 1)
    steering = jnp.dot(one_hot.astype(F32).astype(BF), table[...], preferred_element_type=F32)
    scaled = jnp.sum(jnp.where(one_hot, strength[...], 0.0), axis=1, keepdims=True)
    self_sq = jnp.sum(residual * residual, axis=1, keepdims=True)
    steer_sq = jnp.sum(steering * steering, axis=1, keepdims=True)
    factor = scaled * jnp.sqrt(self_sq / D / (steer_sq / D + 1e-06))
    gained = (residual + factor * steering) * gain[...]
    totals = jnp.sum(gained * gained, axis=1, keepdims=True)
    out[...] = (gained * lax.rsqrt(totals + 1e-06)).astype(BF)


def embed(*args):
    return pl.pallas_call(
        embed_kernel,
        in_specs=[VM] * 9,
        out_specs=VM,
        out_shape=jax.ShapeDtypeStruct((8, D), BF),
        compiler_params=pltpu.CompilerParams(vmem_limit_bytes=8 << 20),
        name="embed",
    )(*args)


def score(groups, pieces, index_rows, out=None):
    n_rows = sum(p.shape[0] for p in pieces)
    n_groups = n_rows // QRY
    index_count = index_rows.shape[0]
    block = 256
    steps = index_count // block

    def kernel(*refs):
        group = refs[0]
        piece_refs = refs[1 : 1 + len(pieces)]
        index_ref = refs[1 + len(pieces)]
        target, result, sems = refs[-3], refs[-2], refs[-1]
        step = pl.program_id(0)
        rows = jnp.concatenate([p[...] for p in piece_refs], axis=0)
        result[step] = lax.dot_general(
            rows, index_ref[...], (((1,), (1,)), ((), ())), preferred_element_type=F32
        ).astype(BF)

        def copy(i, n):
            first = pl.multiple_of(group[n] * QRY, QRY)
            return pltpu.make_async_copy(
                result.at[i, pl.ds(n * QRY, QRY)],
                target.at[pl.ds(first, QRY), pl.ds(pl.multiple_of(i * block, block), block)],
                sems.at[i, n],
            )

        for n in range(n_groups):
            copy(step, n).start()

        @pl.when(step == steps - 1)
        def _():
            for i in range(steps):
                for n in range(n_groups):
                    copy(i, n).wait()

    specs = [SM] + [VM] * len(pieces) + [pl.BlockSpec((block, D), lambda i: (i, 0))]
    args = [groups, *pieces, index_rows]
    alias = {}
    if out is not None:
        specs.append(ANY)
        args.append(out)
        alias = {len(args) - 1: 0}
    return pl.pallas_call(
        kernel,
        grid=(steps,),
        in_specs=specs,
        out_specs=ANY,
        out_shape=jax.ShapeDtypeStruct((1024, index_count), BF),
        scratch_shapes=[
            pltpu.VMEM((steps, n_rows, block), BF),
            pltpu.SemaphoreType.DMA((steps, n_groups)),
        ],
        input_output_aliases=alias,
        compiler_params=pltpu.CompilerParams(vmem_limit_bytes=20 << 20),
        name="score",
    )(*args)


def on_device(
    hidden,
    lengths,
    steer_ids,
    in_gain,
    w_query,
    w_key,
    w_value,
    w_out,
    steer_table,
    strength,
    out_gain,
    index_rows,
):
    x = lax.axis_index("tensor")
    corpus = lax.axis_index("corpus")
    y, z, core = corpus // 8, (corpus // 2) % 4, corpus % 2

    left = lax.ppermute(hidden, "tensor", ring(1))
    right = lax.ppermute(hidden, "tensor", ring(-1))
    far_top = lax.ppermute(left[: TOK // 2], "tensor", ring(1))
    far_low = lax.ppermute(right[TOK // 2 :], "tensor", ring(-1))

    counts = lengths[0]
    order = jnp.arange(QRY, dtype=jnp.int32)
    ends = jnp.sum(jnp.where(order[None, :] <= order[:, None], counts[None, :], 0), axis=1)
    starts = ends - counts
    tokens = jnp.arange(TOK, dtype=jnp.int32)
    opened = jnp.max(jnp.where(starts[None, :] <= tokens[:, None], starts[None, :], 0), axis=1)
    tables = rotary(tokens - opened) + rotary(counts - 1)
    my_ends = lax.dynamic_slice(ends, (x * 8,), (8,))
    my_ids = lax.dynamic_slice(steer_ids, (x * 8,), (8,))
    meta = jnp.stack([x, (x + 3) % 4, (x + 1) % 4, (x + 2) % 4, x]).astype(jnp.int32)

    part0, part1, part2, part3, pooled_x = encode(
        meta,
        (hidden, left, right, far_top, far_low),
        in_gain.reshape(4, D // 4),
        tables,
        (starts[:, None], ends[:, None], my_ends[:, None]),
        (w_query, w_key, w_value, w_out),
    )
    part1 = lax.ppermute(part1, "tensor", ring(1))
    part3 = lax.ppermute(part3, "tensor", ring(3))
    part2 = lax.ppermute(part2, "tensor", ring(2))
    mine = embed(
        part0,
        part1,
        part2,
        part3,
        pooled_x,
        my_ids[:, None],
        steer_table,
        strength[None, :],
        out_gain[None, :],
    )

    shifts = [mine] + [lax.ppermute(mine, "tensor", ring(k)) for k in (1, 3, 2)]
    shifts = [shifts[0], shifts[1], shifts[3], shifts[2]]
    rows = jnp.concatenate(
        [lax.select_n((x + 4 - s) % 4, *shifts) for s in range(4)], axis=0
    )

    near = [lax.ppermute(rows, "corpus", planes(True, k)) for k in (1, 3, 2)]
    line = jnp.concatenate([rows, near[0], near[2], near[1]], axis=0)
    below = lax.ppermute(line, "corpus", planes(False, 1))
    above = lax.ppermute(line, "corpus", planes(False, 3))
    top = lax.ppermute(below[:64], "corpus", planes(False, 1))
    low = lax.ppermute(above[64:], "corpus", planes(False, 3))

    def swap(a):
        return lax.ppermute(a, "corpus", partners())

    other = [swap(a) for a in (line, below, above, top, low)]

    def groups(of_core, ks, m):
        first, second = (y, z), (z, y)
        ks = jnp.asarray(ks, jnp.int32)
        along = (jnp.where(of_core == 0, y, z) + 4 - ks) % 4
        across = (jnp.where(of_core == 0, z, y) + 4 - m) % 4
        at_y = jnp.where(of_core == 0, along, across)
        at_z = jnp.where(of_core == 0, across, along)
        return ((at_y * 4 + at_z) * 2 + of_core).astype(jnp.int32)

    slots = (0, 1, 2, 3)
    peer = 1 - core
    g1 = jnp.concatenate([groups(core, slots, 0), groups(peer, slots, 0)])
    g2 = jnp.concatenate(
        [groups(core, slots, 1), groups(core, slots, 3), groups(peer, slots, 1), groups(peer, slots, 3)]
    )
    g3 = jnp.concatenate([groups(core, slots, 2), groups(peer, slots, 2)])
    out = score(g1, [line, other[0]], index_rows)
    out = score(g2, [below, above, other[1], other[2]], index_rows, out)
    return score(g3, [top, low, other[3], other[4]], index_rows, out)


def solution(mesh):
    placed = (
        P("corpus", "tensor"),
        P("corpus", None),
        P("corpus"),
        P(),
        P(None, "tensor"),
        P(None, "tensor"),
        P(None, "tensor"),
        P("tensor", None),
        P(),
        P(),
        P(),
        P(("corpus", "tensor"), None),
    )
    return jax.shard_map(
        on_device,
        mesh=mesh,
        in_specs=placed,
        out_specs=P(None, ("corpus", "tensor")),
        check_vma=False,
    )
```

```python
import jax
import jax.numpy as jnp
from jax import lax
from jax.experimental import pallas as pl
from jax.experimental.pallas import tpu as pltpu
from jax.sharding import PartitionSpec as P

D = 4096
HEAD = 128
TOK = 384
QRY = 32
ROPE_BASE = 1000000.0
BF = jnp.bfloat16
F32 = jnp.float32


VM = pl.BlockSpec(memory_space=pltpu.VMEM)
SM = pl.BlockSpec(memory_space=pltpu.SMEM)
ANY = pl.BlockSpec(memory_space=pl.ANY)
HBM = pl.BlockSpec(memory_space=pltpu.HBM)


def pinned(a):
    return pltpu.with_memory_space_constraint(a, pltpu.HBM)


def ring(k):
    return [(i, (i + k) % 4) for i in range(4)]


def spot(y, z, core):
    return ((y % 4) * 4 + z % 4) * 2 + core


def planes(first, k):
    pairs = []
    for y in range(4):
        for z in range(4):
            for core in range(2):
                along_y = (core == 0) == first
                target = spot(y + k, z, core) if along_y else spot(y, z + k, core)
                pairs.append((spot(y, z, core), target))
    return pairs


def partners():
    return [(i, i ^ 1) for i in range(32)]


def rotary(positions):
    half = HEAD // 2
    frequency = ROPE_BASE ** (-(jnp.arange(half, dtype=F32) * 2.0) / HEAD)
    frequency = jnp.concatenate([frequency, frequency])
    sign = jnp.where(jnp.arange(HEAD) < half, -1.0, 1.0).astype(F32)
    angles = positions.astype(F32)[:, None] * frequency[None, :]
    return jnp.cos(angles), jnp.sin(angles) * sign[None, :]


def encode_kernel(
    meta,
    own,
    left,
    right,
    far_top,
    far_low,
    gain,
    cos_k,
    sin_k,
    cos_q,
    sin_q,
    starts,
    ends,
    my_ends,
    wq_hbm,
    wk_hbm,
    wv_hbm,
    wo_hbm,
    part0,
    part1,
    part2,
    part3,
    pooled_x,
    normed,
    wq,
    wk,
    wv,
    wo,
    context,
    summed,
    sems,
):
    width = own.shape[1]
    copies = []
    for i, (source, target) in enumerate(((wk_hbm, wk), (wv_hbm, wv), (wq_hbm, wq))):
        for j in range(4):
            rows = pl.ds(pl.multiple_of(meta[j] * width, width), width)
            copies.append(
                pltpu.make_async_copy(source.at[rows], target.at[pl.ds(j * width, width)], sems.at[i * 4 + j])
            )
    copies.append(pltpu.make_async_copy(wo_hbm, wo, sems.at[12]))
    for copy in copies:
        copy.start()

    chunk = 64
    for base in range(0, TOK, chunk):
        if base < TOK // 2:
            far, far_base = far_top, base
        else:
            far, far_base = far_low, base - TOK // 2
        blocks = [(own, base), (left, base), (right, base), (far, far_base)]
        acc = jnp.zeros((chunk, 128), F32)
        for ref, start in blocks:
            for lane in range(0, width, 128):
                x = ref[start : start + chunk, lane : lane + 128].astype(F32)
                acc = acc + x * x
        scale = lax.rsqrt(jnp.sum(acc, axis=1, keepdims=True) / D + 1e-06)
        for j, (ref, start) in enumerate(blocks):
            x = ref[start : start + chunk, :].astype(F32)
            row = gain[pl.ds(meta[j], 1), :]
            normed[base : base + chunk, j * width : (j + 1) * width] = (x * scale * row).astype(BF)

    tokens = lax.broadcasted_iota(jnp.int32, (QRY, TOK), 1)
    visible = (tokens >= starts[...]) & (tokens < ends[...])
    pick = (tokens == ends[...] - 1).astype(F32).astype(BF)

    half_tokens = lax.broadcasted_iota(jnp.int32, (8, TOK // 2), 1)
    last8 = my_ends[...] - 1
    pick8_top = (half_tokens == last8).astype(F32).astype(BF)
    pick8_low = (half_tokens + TOK // 2 == last8).astype(F32).astype(BF)
    half = TOK // 2
    raw = [
        (own[0:half, :], own[half:TOK, :]),
        (left[0:half, :], left[half:TOK, :]),
        (right[0:half, :], right[half:TOK, :]),
        (far_top[...], far_low[...]),
    ]
    for j, (top, low) in enumerate(raw):
        rows = jnp.dot(pick8_top, top, preferred_element_type=F32) + jnp.dot(
            pick8_low, low, preferred_element_type=F32
        )
        pooled_x[:, pl.ds(pl.multiple_of(meta[j] * width, width), width)] = rows

    for copy in copies[0:4]:
        copy.wait()
    keys = jnp.dot(normed[...], wk[...], preferred_element_type=F32)
    for copy in copies[4:8]:
        copy.wait()
    values = jnp.dot(normed[...], wv[...], preferred_element_type=F32).astype(BF)
    pooled = jnp.dot(pick, normed[...], preferred_element_type=F32).astype(BF)
    for copy in copies[8:12]:
        copy.wait()
    queries = jnp.dot(pooled, wq[...], preferred_element_type=F32)

    def turn(v, cosine, sine):
        return (v * cosine + pltpu.roll(v, HEAD // 2, 1) * sine).astype(BF)

    for g in range(2):
        lanes = slice(g * HEAD, (g + 1) * HEAD)
        key = turn(keys[:, lanes], cos_k[...], sin_k[...])
        value = values[:, lanes]
        for r in range(2):
            h = 2 * g + r
            heads = slice(h * HEAD, (h + 1) * HEAD)
            query = turn(queries[:, heads], cos_q[...], sin_q[...])
            scores = lax.dot_general(
                query, key, (((1,), (1,)), ((), ())), preferred_element_type=F32
            ) * HEAD ** (-0.5)
            scores = jnp.where(visible, scores, -1e30)
            weights = jnp.exp(scores - jnp.max(scores, axis=1, keepdims=True))
            probs = (weights / jnp.sum(weights, axis=1, keepdims=True)).astype(BF)
            context[:, heads] = jnp.dot(probs, value, preferred_element_type=F32).astype(BF)

    copies[12].wait()
    summed[...] = jnp.dot(context[...], wo[...], preferred_element_type=F32)
    for k, part in enumerate((part0, part1, part2, part3)):
        first = lax.rem(meta[4] + k, 4) * 8
        part[...] = summed[pl.ds(pl.multiple_of(first, 8), 8), :]


def encode(meta, blocks, gain, tables, bounds, weights):
    rows = jax.ShapeDtypeStruct((8, D), F32)
    return pl.pallas_call(
        encode_kernel,
        in_specs=[SM] + [VM] * 5 + [VM] + [VM] * 4 + [VM] * 3 + [HBM] * 4,
        out_specs=[VM] * 5,
        out_shape=[rows] * 5,
        scratch_shapes=[
            pltpu.VMEM((TOK, D), BF),
            pltpu.VMEM((D, 512), BF),
            pltpu.VMEM((D, 256), BF),
            pltpu.VMEM((D, 256), BF),
            pltpu.VMEM((512, D), BF),
            pltpu.VMEM((QRY, 512), BF),
            pltpu.VMEM((QRY, D), F32),
            pltpu.SemaphoreType.DMA((13,)),
        ],
        compiler_params=pltpu.CompilerParams(vmem_limit_bytes=36 << 20),
        name="encode",
    )(meta, *blocks, gain, *tables, *bounds, *weights)


def embed_kernel(part0, part1, part2, part3, pooled_x, ids, table, strength, gain, out):
    residual = pooled_x[...] + ((part0[...] + part1[...]) + (part2[...] + part3[...]))
    one_hot = ids[...] == lax.broadcasted_iota(jnp.int32, (8, 16), 1)
    steering = jnp.dot(one_hot.astype(F32).astype(BF), table[...], preferred_element_type=F32)
    scaled = jnp.sum(jnp.where(one_hot, strength[...], 0.0), axis=1, keepdims=True)
    self_sq = jnp.sum(residual * residual, axis=1, keepdims=True)
    steer_sq = jnp.sum(steering * steering, axis=1, keepdims=True)
    factor = scaled * jnp.sqrt(self_sq / D / (steer_sq / D + 1e-06))
    gained = (residual + factor * steering) * gain[...]
    totals = jnp.sum(gained * gained, axis=1, keepdims=True)
    out[...] = (gained * lax.rsqrt(totals + 1e-06)).astype(BF)


def embed(*args):
    return pl.pallas_call(
        embed_kernel,
        in_specs=[VM] * 9,
        out_specs=VM,
        out_shape=jax.ShapeDtypeStruct((8, D), BF),
        compiler_params=pltpu.CompilerParams(vmem_limit_bytes=8 << 20),
        name="embed",
    )(*args)


def score(groups, pieces, index_rows, out=None):
    n_rows = sum(p.shape[0] for p in pieces)
    n_groups = n_rows // QRY
    index_count = index_rows.shape[0]
    block = 256
    steps = index_count // block

    def kernel(*refs):
        group = refs[0]
        piece_refs = refs[1 : 1 + len(pieces)]
        index_ref = refs[1 + len(pieces)]
        target, result, held, sems, load_sems = refs[-5:]

        def load(i):
            return pltpu.make_async_copy(
                index_ref.at[pl.ds(i * block, block)], held.at[i], load_sems.at[i]
            )

        def copy(i, n):
            first = pl.multiple_of(group[n] * QRY, QRY)
            return pltpu.make_async_copy(
                result.at[i, pl.ds(n * QRY, QRY)],
                target.at[pl.ds(first, QRY), pl.ds(i * block, block)],
                sems.at[i, n],
            )

        for i in range(steps):
            load(i).start()
        rows = jnp.concatenate([p[...] for p in piece_refs], axis=0)
        for i in range(steps):
            load(i).wait()
            result[i] = lax.dot_general(
                rows, held[i], (((1,), (1,)), ((), ())), preferred_element_type=F32
            ).astype(BF)
            for n in range(n_groups):
                copy(i, n).start()
        for i in range(steps):
            for n in range(n_groups):
                copy(i, n).wait()

    specs = [SM] + [VM] * len(pieces) + [HBM]
    args = [groups, *pieces, pinned(index_rows)]
    alias = {}
    if out is not None:
        specs.append(ANY)
        args.append(out)
        alias = {len(args) - 1: 0}
    return pl.pallas_call(
        kernel,
        in_specs=specs,
        out_specs=ANY,
        out_shape=jax.ShapeDtypeStruct((1024, index_count), BF),
        scratch_shapes=[
            pltpu.VMEM((steps, n_rows, block), BF),
            pltpu.VMEM((steps, block, D), BF),
            pltpu.SemaphoreType.DMA((steps, n_groups)),
            pltpu.SemaphoreType.DMA((steps,)),
        ],
        input_output_aliases=alias,
        compiler_params=pltpu.CompilerParams(vmem_limit_bytes=20 << 20),
        name="score",
    )(*args)


def on_device(
    hidden,
    lengths,
    steer_ids,
    in_gain,
    w_query,
    w_key,
    w_value,
    w_out,
    steer_table,
    strength,
    out_gain,
    index_rows,
):
    x = lax.axis_index("tensor")
    corpus = lax.axis_index("corpus")
    y, z, core = corpus // 8, (corpus // 2) % 4, corpus % 2

    left = lax.ppermute(hidden, "tensor", ring(1))
    right = lax.ppermute(hidden, "tensor", ring(-1))
    far_top = lax.ppermute(left[: TOK // 2], "tensor", ring(1))
    far_low = lax.ppermute(right[TOK // 2 :], "tensor", ring(-1))

    counts = lengths[0]
    order = jnp.arange(QRY, dtype=jnp.int32)
    ends = jnp.sum(jnp.where(order[None, :] <= order[:, None], counts[None, :], 0), axis=1)
    starts = ends - counts
    tokens = jnp.arange(TOK, dtype=jnp.int32)
    opened = jnp.max(jnp.where(starts[None, :] <= tokens[:, None], starts[None, :], 0), axis=1)
    tables = rotary(tokens - opened) + rotary(counts - 1)
    my_ends = lax.dynamic_slice(ends, (x * 8,), (8,))
    my_ids = lax.dynamic_slice(steer_ids, (x * 8,), (8,))
    meta = jnp.stack([x, (x + 3) % 4, (x + 1) % 4, (x + 2) % 4, x]).astype(jnp.int32)

    part0, part1, part2, part3, pooled_x = encode(
        meta,
        (hidden, left, right, far_top, far_low),
        in_gain.reshape(4, D // 4),
        tables,
        (starts[:, None], ends[:, None], my_ends[:, None]),
        tuple(pinned(w) for w in (w_query, w_key, w_value, w_out)),
    )
    part1 = lax.ppermute(part1, "tensor", ring(1))
    part3 = lax.ppermute(part3, "tensor", ring(3))
    part2 = lax.ppermute(part2, "tensor", ring(2))
    mine = embed(
        part0,
        part1,
        part2,
        part3,
        pooled_x,
        my_ids[:, None],
        steer_table,
        strength[None, :],
        out_gain[None, :],
    )

    shifts = [mine] + [lax.ppermute(mine, "tensor", ring(k)) for k in (1, 3, 2)]
    shifts = [shifts[0], shifts[1], shifts[3], shifts[2]]
    rows = jnp.concatenate(
        [lax.select_n((x + 4 - s) % 4, *shifts) for s in range(4)], axis=0
    )

    near = [lax.ppermute(rows, "corpus", planes(True, k)) for k in (1, 3, 2)]
    early = jnp.concatenate([rows, near[0]], axis=0)
    below_early = lax.ppermute(early, "corpus", planes(False, 1))
    above_early = lax.ppermute(early, "corpus", planes(False, 3))
    late = jnp.concatenate([near[1], near[2]], axis=0)
    below_late = lax.ppermute(late, "corpus", planes(False, 1))
    above_late = lax.ppermute(late, "corpus", planes(False, 3))

    def swap(a):
        return lax.ppermute(a, "corpus", partners())

    def groups(of_core, ks, m):
        first, second = (y, z), (z, y)
        ks = jnp.asarray(ks, jnp.int32)
        along = (jnp.where(of_core == 0, y, z) + 4 - ks) % 4
        across = (jnp.where(of_core == 0, z, y) + 4 - m) % 4
        at_y = jnp.where(of_core == 0, along, across)
        at_z = jnp.where(of_core == 0, across, along)
        return ((at_y * 4 + at_z) * 2 + of_core).astype(jnp.int32)

    slots = (0, 1, 3, 2)
    peer = 1 - core
    g1 = jnp.concatenate([groups(core, slots, 0), groups(peer, slots, 0)])
    g2 = jnp.concatenate(
        [groups(c, ks, m) for c in (core, peer) for ks in ((0, 1), (3, 2)) for m in (1, 3)]
    )
    g3 = jnp.concatenate([groups(core, slots, 2), groups(peer, slots, 2)])
    out = score(g1, [early, late, swap(early), swap(late)], index_rows)
    below_early, out = lax.optimization_barrier((below_early, out))
    far_early = lax.ppermute(below_early, "corpus", planes(False, 1))
    far_late = lax.ppermute(above_late, "corpus", planes(False, 3))
    second = [below_early, above_early, below_late, above_late]
    out = score(g2, second + [swap(a) for a in second], index_rows, out)
    far_early, far_late, out = lax.optimization_barrier((far_early, far_late, out))
    return score(g3, [far_early, far_late, swap(far_early), swap(far_late)], index_rows, out)


def solution(mesh):
    placed = (
        P("corpus", "tensor"),
        P("corpus", None),
        P("corpus"),
        P(),
        P(None, "tensor"),
        P(None, "tensor"),
        P(None, "tensor"),
        P("tensor", None),
        P(),
        P(),
        P(),
        P(("corpus", "tensor"), None),
    )
    return jax.shard_map(
        on_device,
        mesh=mesh,
        in_specs=placed,
        out_specs=P(None, ("corpus", "tensor")),
        check_vma=False,
    )
```

```python
import jax
import jax.numpy as jnp
from jax import lax
from jax.experimental import pallas as pl
from jax.experimental.pallas import tpu as pltpu
from jax.sharding import PartitionSpec as P

D = 4096
HEAD = 128
TOK = 384
QRY = 32
ROPE_BASE = 1000000.0
BF = jnp.bfloat16
F32 = jnp.float32


VM = pl.BlockSpec(memory_space=pltpu.VMEM)
SM = pl.BlockSpec(memory_space=pltpu.SMEM)
ANY = pl.BlockSpec(memory_space=pl.ANY)
HBM = pl.BlockSpec(memory_space=pltpu.HBM)


def pinned(a):
    return pltpu.with_memory_space_constraint(a, pltpu.HBM)


def in_vmem(a):
    return pltpu.with_memory_space_constraint(a, pltpu.VMEM)


def ring(k):
    return [(i, (i + k) % 4) for i in range(4)]


def spot(y, z, core):
    return ((y % 4) * 4 + z % 4) * 2 + core


def planes(first, k):
    pairs = []
    for y in range(4):
        for z in range(4):
            for core in range(2):
                along_y = (core == 0) == first
                target = spot(y + k, z, core) if along_y else spot(y, z + k, core)
                pairs.append((spot(y, z, core), target))
    return pairs


def partners():
    return [(i, i ^ 1) for i in range(32)]


def rotary(positions):
    half = HEAD // 2
    frequency = ROPE_BASE ** (-(jnp.arange(half, dtype=F32) * 2.0) / HEAD)
    frequency = jnp.concatenate([frequency, frequency])
    sign = jnp.where(jnp.arange(HEAD) < half, -1.0, 1.0).astype(F32)
    angles = positions.astype(F32)[:, None] * frequency[None, :]
    return jnp.cos(angles), jnp.sin(angles) * sign[None, :]


def stage_kernel(meta, wq_hbm, wk_hbm, wv_hbm, wo_hbm, wq, wk, wv, wo, sems):
    width = D // 4
    copies = []
    for i, (source, target) in enumerate(((wk_hbm, wk), (wv_hbm, wv), (wq_hbm, wq))):
        for j in range(4):
            rows = pl.ds(pl.multiple_of(meta[j] * width, width), width)
            copies.append(
                pltpu.make_async_copy(source.at[rows], target.at[pl.ds(j * width, width)], sems.at[i * 4 + j])
            )
    copies.append(pltpu.make_async_copy(wo_hbm, wo, sems.at[12]))
    for copy in copies:
        copy.start()
    for copy in copies:
        copy.wait()


def stage(meta, arrays):
    return pl.pallas_call(
        stage_kernel,
        in_specs=[SM] + [HBM] * 4,
        out_specs=[VM] * 4,
        out_shape=[pltpu.VMEM(a.shape, a.dtype) for a in arrays],
        scratch_shapes=[pltpu.SemaphoreType.DMA((13,))],
        compiler_params=pltpu.CompilerParams(vmem_limit_bytes=2 << 20),
        name="stage",
    )(meta, *[pinned(a) for a in arrays])


CHUNK = 64


def squares(ref, start, acc):
    for lane in range(0, ref.shape[1], 128):
        x = ref[start : start + CHUNK, lane : lane + 128].astype(F32)
        acc = acc + x * x
    return acc


def picked(last, top, low):
    half = TOK // 2
    tokens = lax.broadcasted_iota(jnp.int32, (last.shape[0], half), 1)
    pick_top = (tokens == last).astype(F32).astype(BF)
    pick_low = (tokens + half == last).astype(F32).astype(BF)
    return jnp.dot(pick_top, top, preferred_element_type=F32) + jnp.dot(
        pick_low, low, preferred_element_type=F32
    )


def early_kernel(own, left, right, my_ends, sums, rows):
    half = TOK // 2
    for base in range(0, TOK, CHUNK):
        acc = jnp.zeros((CHUNK, 128), F32)
        for ref in (own, left, right):
            acc = squares(ref, base, acc)
        sums[base : base + CHUNK, :] = acc
    for j, ref in enumerate((own, left, right)):
        rows[:, j * 1024 : (j + 1) * 1024] = picked(my_ends[...] - 1, ref[0:half, :], ref[half:TOK, :])


def early_part(own, left, right, my_ends):
    return pl.pallas_call(
        early_kernel,
        in_specs=[VM] * 4,
        out_specs=[VM] * 2,
        out_shape=[jax.ShapeDtypeStruct((TOK, 128), F32), jax.ShapeDtypeStruct((8, 3 * D // 4), F32)],
        compiler_params=pltpu.CompilerParams(vmem_limit_bytes=6 << 20),
        name="early",
    )(own, left, right, my_ends)


def encode_kernel(
    meta,
    own,
    left,
    right,
    far_top,
    far_low,
    sums,
    gain,
    cos_k,
    sin_k,
    cos_q,
    sin_q,
    starts,
    ends,
    wq,
    wk,
    wv,
    wo,
    part0,
    part1,
    part2,
    part3,
    normed,
    context,
    summed,
):
    width = own.shape[1]
    for base in range(0, TOK, CHUNK):
        if base < TOK // 2:
            far, far_base = far_top, base
        else:
            far, far_base = far_low, base - TOK // 2
        acc = squares(far, far_base, sums[base : base + CHUNK, :])
        scale = lax.rsqrt(jnp.sum(acc, axis=1, keepdims=True) / D + 1e-06)
        for j, (ref, start) in enumerate(((own, base), (left, base), (right, base), (far, far_base))):
            x = ref[start : start + CHUNK, :].astype(F32)
            row = gain[pl.ds(meta[j], 1), :]
            normed[base : base + CHUNK, j * width : (j + 1) * width] = (x * scale * row).astype(BF)

    tokens = lax.broadcasted_iota(jnp.int32, (QRY, TOK), 1)
    visible = (tokens >= starts[...]) & (tokens < ends[...])
    pick = (tokens == ends[...] - 1).astype(F32).astype(BF)
    pooled = jnp.dot(pick, normed[...], preferred_element_type=F32).astype(BF)
    queries = jnp.dot(pooled, wq[...], preferred_element_type=F32)
    keys = jnp.dot(normed[...], wk[...], preferred_element_type=F32)
    values = jnp.dot(normed[...], wv[...], preferred_element_type=F32).astype(BF)

    def turn(v, cosine, sine):
        return (v * cosine + pltpu.roll(v, HEAD // 2, 1) * sine).astype(BF)

    for g in range(2):
        lanes = slice(g * HEAD, (g + 1) * HEAD)
        key = turn(keys[:, lanes], cos_k[...], sin_k[...])
        value = values[:, lanes]
        for r in range(2):
            h = 2 * g + r
            heads = slice(h * HEAD, (h + 1) * HEAD)
            query = turn(queries[:, heads], cos_q[...], sin_q[...])
            scores = lax.dot_general(
                query, key, (((1,), (1,)), ((), ())), preferred_element_type=F32
            ) * HEAD ** (-0.5)
            scores = jnp.where(visible, scores, -1e30)
            weights = jnp.exp(scores - jnp.max(scores, axis=1, keepdims=True))
            probs = (weights / jnp.sum(weights, axis=1, keepdims=True)).astype(BF)
            context[:, heads] = jnp.dot(probs, value, preferred_element_type=F32).astype(BF)

    summed[...] = jnp.dot(context[...], wo[...], preferred_element_type=F32)
    for k, part in enumerate((part0, part1, part2, part3)):
        first = lax.rem(meta[4] + k, 4) * 8
        part[...] = summed[pl.ds(pl.multiple_of(first, 8), 8), :]


def encode(meta, blocks, sums, gain, tables, bounds, weights):
    rows = jax.ShapeDtypeStruct((8, D), F32)
    return pl.pallas_call(
        encode_kernel,
        in_specs=[SM] + [VM] * 17,
        out_specs=[VM] * 4,
        out_shape=[rows] * 4,
        scratch_shapes=[
            pltpu.VMEM((TOK, D), BF),
            pltpu.VMEM((QRY, 512), BF),
            pltpu.VMEM((QRY, D), F32),
        ],
        compiler_params=pltpu.CompilerParams(vmem_limit_bytes=16 << 20),
        name="encode",
    )(meta, *blocks, sums, gain, *tables, *bounds, *[in_vmem(w) for w in weights])


def embed_kernel(
    meta,
    part0,
    part1,
    part2,
    part3,
    rows,
    far_top,
    far_low,
    my_ends,
    ids,
    table,
    strength,
    gain,
    out,
    pooled_x,
):
    width = D // 4
    for j in range(3):
        lanes = pl.ds(pl.multiple_of(meta[j] * width, width), width)
        pooled_x[:, lanes] = rows[:, j * width : (j + 1) * width]
    lanes = pl.ds(pl.multiple_of(meta[3] * width, width), width)
    pooled_x[:, lanes] = picked(my_ends[...] - 1, far_top[...], far_low[...])
    residual = pooled_x[...] + ((part0[...] + part1[...]) + (part2[...] + part3[...]))
    one_hot = ids[...] == lax.broadcasted_iota(jnp.int32, (8, 16), 1)
    steering = jnp.dot(one_hot.astype(F32).astype(BF), table[...], preferred_element_type=F32)
    scaled = jnp.sum(jnp.where(one_hot, strength[...], 0.0), axis=1, keepdims=True)
    self_sq = jnp.sum(residual * residual, axis=1, keepdims=True)
    steer_sq = jnp.sum(steering * steering, axis=1, keepdims=True)
    factor = scaled * jnp.sqrt(self_sq / D / (steer_sq / D + 1e-06))
    gained = (residual + factor * steering) * gain[...]
    totals = jnp.sum(gained * gained, axis=1, keepdims=True)
    out[...] = (gained * lax.rsqrt(totals + 1e-06)).astype(BF)


def embed(*args):
    return pl.pallas_call(
        embed_kernel,
        in_specs=[SM] + [VM] * 12,
        out_specs=VM,
        out_shape=jax.ShapeDtypeStruct((8, D), BF),
        scratch_shapes=[pltpu.VMEM((8, D), F32)],
        compiler_params=pltpu.CompilerParams(vmem_limit_bytes=8 << 20),
        name="embed",
    )(*args)


def score(groups, pieces, index_rows, out=None):
    n_rows = sum(p.shape[0] for p in pieces)
    n_groups = n_rows // QRY
    index_count = index_rows.shape[0]
    block = 512
    steps = index_count // block

    def kernel(*refs):
        group = refs[0]
        piece_refs = refs[1 : 1 + len(pieces)]
        index_ref = refs[1 + len(pieces)]
        target, rows, result, sems = refs[-4:]
        step = pl.program_id(0)

        @pl.when(step == 0)
        def _():
            first = 0
            for piece in piece_refs:
                rows[first : first + piece.shape[0], :] = piece[...]
                first += piece.shape[0]

        result[step] = lax.dot_general(
            rows[...], index_ref[...], (((1,), (1,)), ((), ())), preferred_element_type=F32
        ).astype(BF)

        def copy(i, n):
            first = pl.multiple_of(group[n] * QRY, QRY)
            return pltpu.make_async_copy(
                result.at[i, pl.ds(n * QRY, QRY)],
                target.at[pl.ds(first, QRY), pl.ds(pl.multiple_of(i * block, block), block)],
                sems.at[i, n],
            )

        for n in range(n_groups):
            copy(step, n).start()

        @pl.when(step == steps - 1)
        def _():
            for i in range(steps):
                for n in range(n_groups):
                    copy(i, n).wait()

    specs = [SM] + [VM] * len(pieces) + [pl.BlockSpec((block, D), lambda i: (i, 0))]
    args = [groups, *pieces, pinned(index_rows)]
    alias = {}
    if out is not None:
        specs.append(ANY)
        args.append(out)
        alias = {len(args) - 1: 0}
    return pl.pallas_call(
        kernel,
        grid=(steps,),
        in_specs=specs,
        out_specs=ANY,
        out_shape=jax.ShapeDtypeStruct((1024, index_count), BF),
        scratch_shapes=[
            pltpu.VMEM((n_rows, D), BF),
            pltpu.VMEM((steps, n_rows, block), BF),
            pltpu.SemaphoreType.DMA((steps, n_groups)),
        ],
        input_output_aliases=alias,
        compiler_params=pltpu.CompilerParams(vmem_limit_bytes=20 << 20),
        name="score",
    )(*args)


def on_device(
    hidden,
    lengths,
    steer_ids,
    in_gain,
    w_query,
    w_key,
    w_value,
    w_out,
    steer_table,
    strength,
    out_gain,
    index_rows,
):
    x = lax.axis_index("tensor")
    corpus = lax.axis_index("corpus")
    y, z, core = corpus // 8, (corpus // 2) % 4, corpus % 2

    left = lax.ppermute(hidden, "tensor", ring(1))
    right = lax.ppermute(hidden, "tensor", ring(-1))
    far_top = lax.ppermute(left[: TOK // 2], "tensor", ring(1))
    far_low = lax.ppermute(right[TOK // 2 :], "tensor", ring(-1))

    counts = lengths[0]
    order = jnp.arange(QRY, dtype=jnp.int32)
    ends = jnp.sum(jnp.where(order[None, :] <= order[:, None], counts[None, :], 0), axis=1)
    starts = ends - counts
    tokens = jnp.arange(TOK, dtype=jnp.int32)
    opened = jnp.max(jnp.where(starts[None, :] <= tokens[:, None], starts[None, :], 0), axis=1)
    tables = rotary(tokens - opened) + rotary(counts - 1)
    my_ends = lax.dynamic_slice(ends, (x * 8,), (8,))
    my_ids = lax.dynamic_slice(steer_ids, (x * 8,), (8,))
    meta = jnp.stack([x, (x + 3) % 4, (x + 1) % 4, (x + 2) % 4, x]).astype(jnp.int32)

    weights = stage(meta, (w_query, w_key, w_value, w_out))
    sums, early_rows = early_part(hidden, left, right, my_ends[:, None])
    part0, part1, part2, part3 = encode(
        meta,
        (hidden, left, right, far_top, far_low),
        sums,
        in_gain.reshape(4, D // 4),
        tables,
        (starts[:, None], ends[:, None]),
        weights,
    )
    part1 = lax.ppermute(part1, "tensor", ring(1))
    part3 = lax.ppermute(part3, "tensor", ring(3))
    part2 = lax.ppermute(part2, "tensor", ring(2))
    mine = embed(
        meta,
        part0,
        part1,
        part2,
        part3,
        early_rows,
        far_top,
        far_low,
        my_ends[:, None],
        my_ids[:, None],
        steer_table,
        strength[None, :],
        out_gain[None, :],
    )

    shifts = [mine] + [lax.ppermute(mine, "tensor", ring(k)) for k in (1, 3, 2)]
    shifts = [shifts[0], shifts[1], shifts[3], shifts[2]]
    rows = jnp.concatenate(
        [lax.select_n((x + 4 - s) % 4, *shifts) for s in range(4)], axis=0
    )

    near = [lax.ppermute(rows, "corpus", planes(True, k)) for k in (1, 3, 2)]
    early = jnp.concatenate([rows, near[0]], axis=0)
    below_early = lax.ppermute(early, "corpus", planes(False, 1))
    above_early = lax.ppermute(early, "corpus", planes(False, 3))
    late = jnp.concatenate([near[1], near[2]], axis=0)
    below_late = lax.ppermute(late, "corpus", planes(False, 1))
    above_late = lax.ppermute(late, "corpus", planes(False, 3))

    def swap(a):
        return lax.ppermute(a, "corpus", partners())

    def groups(of_core, ks, m):
        first, second = (y, z), (z, y)
        ks = jnp.asarray(ks, jnp.int32)
        along = (jnp.where(of_core == 0, y, z) + 4 - ks) % 4
        across = (jnp.where(of_core == 0, z, y) + 4 - m) % 4
        at_y = jnp.where(of_core == 0, along, across)
        at_z = jnp.where(of_core == 0, across, along)
        return ((at_y * 4 + at_z) * 2 + of_core).astype(jnp.int32)

    slots = (0, 1, 3, 2)
    peer = 1 - core
    g1 = jnp.concatenate([groups(core, slots, 0), groups(peer, slots, 0)])
    g2 = jnp.concatenate(
        [groups(c, ks, m) for c in (core, peer) for ks in ((0, 1), (3, 2)) for m in (1, 3)]
    )
    g3 = jnp.concatenate([groups(core, slots, 2), groups(peer, slots, 2)])
    out = score(g1, [early, late, swap(early), swap(late)], index_rows)
    below_early, out = lax.optimization_barrier((below_early, out))
    far_early = lax.ppermute(below_early, "corpus", planes(False, 1))
    far_late = lax.ppermute(above_late, "corpus", planes(False, 3))
    second = [below_early, above_early, below_late, above_late]
    out = score(g2, second + [swap(a) for a in second], index_rows, out)
    far_early, far_late, out = lax.optimization_barrier((far_early, far_late, out))
    return score(g3, [far_early, far_late, swap(far_early), swap(far_late)], index_rows, out)


def solution(mesh):
    placed = (
        P("corpus", "tensor"),
        P("corpus", None),
        P("corpus"),
        P(),
        P(None, "tensor"),
        P(None, "tensor"),
        P(None, "tensor"),
        P("tensor", None),
        P(),
        P(),
        P(),
        P(("corpus", "tensor"), None),
    )
    return jax.shard_map(
        on_device,
        mesh=mesh,
        in_specs=placed,
        out_specs=P(None, ("corpus", "tensor")),
        check_vma=False,
    )
```
